32 devices in a mesh: seq: 8 (over z, x), head: 4 (over y, core).
Axes of the slice: x: 2, y: 2, z: 4, core: 2. Of those that a mesh axis runs over, the one named last changes fastest.
Arguments:
- queries: bfloat16 [1024, 2048], P('seq', 'head'), may hold values from -200 to 200
- keys: bfloat16 [1024, 2048], P('seq', 'head'), may hold values from -6 to 6
- values: bfloat16 [1024, 2048], P('seq', 'head'), may hold values from -6 to 6
- bucket: int32 [1024, 1], replicated, may hold values from 0 to 7; in each aligned block of 128 rows (0 to 127, 128 to 255, ...) at most 24 rows name the same one
- w_out: bfloat16 [2048, 4096], P('head'), may hold values from -0.125 to 0.125
- grad_out: bfloat16 [1024, 4096], P('seq'), may hold values from -6 to 6
Outputs:
- layer_out: bfloat16 [1024, 4096], P('seq', 'head')
- grad_queries: bfloat16 [1024, 2048], P('seq', 'head')
- grad_keys: bfloat16 [1024, 2048], P('seq', 'head')
- grad_values: bfloat16 [1024, 2048], P('seq', 'head')
- grad_weight: float32 [2048, 4096], P('head', 'seq')
The draws below stay inside these ranges and needn't reach their ends.
Inputs may be any that keep to these rules, and one draw needn't show every extreme that they name: Bucket b belongs to the b-th index of seq; buckets b and b-1 are neighbouring tree leaves. Among the tokens of one block of 128 at most 24 share a bucket, and exactly 24 do in some block.
All inputs are finite; a program needn't handle non-finite values.
Results may differ from the reference program's by a relative error of at most 0.012.
Values may be sent and summed in bfloat16 or wider, within the bound.
A program may use at most 128 MiB of HBM per device.

```python
import math
import jax
import jax.numpy as jnp
import numpy as np
from jax import lax

D = 4096
HEADS = 16
HSZ = 128
TOK_DEV = 128
TOKENS = 1024
HD = 2048
CAP = 24
N_SEQ = 8


def query_key(key):
    base = jax.random.fold_in(key, 7)
    first, second = jax.random.split(base, 2)
    shape = (TOKENS, HD)
    keys_part = jnp.clip(jax.random.normal(first, shape, jnp.float32), -6.0, 6.0)
    queries_part = jnp.clip(jax.random.normal(second, shape, jnp.float32), -6.0, 6.0)
    return (queries_part, keys_part)


def draw_queries(key, part):
    return query_key(key)[0].astype(jnp.bfloat16)


def draw_keys(key, part):
    return query_key(key)[1].astype(jnp.bfloat16)


def raised(result, own_key, source, target, blocks, factor):
    def block_of(dim):
        return (jnp.arange(result.shape[dim]) // (result.shape[dim] // blocks)).reshape((-1,) + (1,) * (result.ndim - 1 - dim))

    first = jax.random.permutation(own_key, blocks)[block_of(target)]
    other_side = (block_of(target) + blocks // 2) % blocks
    return jnp.where((block_of(source) == first) | (block_of(source) == other_side), factor * result, result)


def steps_of(stream_key, shape, pieces, least, high):
    def one(position, shards_of):
        heights = jax.random.uniform(jax.random.fold_in(jax.random.fold_in(stream_key, 6), position), (shards_of,), jnp.float32, least / len(pieces), high / len(pieces))
        return jnp.repeat(jnp.exp(heights), shape[position] // shards_of).reshape((-1,) + (1,) * (len(shape) - position - 1))

    level = one(*pieces[0])
    for cut in pieces[1:]:
        level = level * one(*cut)
    return level


def assign_block(stream_key, own, number, rows, count, top, bound, lean):
    order = jax.random.permutation(stream_key, count)
    heavy_load, ordinary = shares(count, rows * top, bound, lean, True), shares(count, rows * top, bound, lean, False)
    places = jnp.arange(count)

    def named(lengths, turn):
        used = int((lengths > 0).sum())
        fixed = max(1, used // 4)
        passed = fixed + (places - fixed + turn * (used - fixed)) % max(1, count - fixed)
        return jnp.zeros((count,), jnp.int32).at[order[jnp.where(places < fixed, places, passed)]].set(jnp.asarray(lengths, jnp.int32))

    lengths = jnp.where(number % 4 == 0, named(heavy_load, number // 4), named(ordinary, number - number // 4 - 1))
    mixed = jax.random.permutation(jax.random.fold_in(own, 3), count)
    giver, sink = mixed[0:count // 2 * 2:2], mixed[1:count // 2 * 2:2]
    slack = jnp.minimum(lengths[giver] - 1, bound - lengths[sink]) // 2
    slack = jnp.where((giver == order[0]) | (sink == order[0]) | (lengths[sink] == 0), 0, jnp.maximum(slack, 0))
    passed = jax.random.randint(jax.random.fold_in(own, 4), (count // 2,), 0, 1 << 20) % (slack + 1)
    lengths = lengths.at[giver].add(-passed).at[sink].add(passed)
    members = jnp.searchsorted(jnp.cumsum(lengths), jnp.arange(rows * top), side="right").astype(jnp.int32)
    table = members.reshape(top, rows).T
    table = table[jax.random.permutation(jax.random.fold_in(own, 1), rows)]
    turn = jax.random.randint(jax.random.fold_in(own, 2), (rows, 1), 0, top)
    return jnp.take_along_axis(table, (jnp.arange(top)[None, :] + turn) % top, axis=1)


def shares(number_of, total, bound, skew, full):
    weights = [(1 << 20) // math.isqrt(rank ** skew) + 1 for rank in range(1, number_of + 1)]
    largest = bound if full else min(bound, max(-(-total // number_of), total * weights[0] // sum(weights)))
    least = 1 if total - largest >= number_of - 1 else 0
    holding, spare = [largest] + [least] * (number_of - 1), total - largest - least * (number_of - 1)
    while spare > 0:
        movable = [i for i in range(1, number_of) if holding[i] < largest] or [i for i in range(1, number_of) if holding[i] < bound]
        whole, remaining = sum([weights[i] for i in movable]), spare
        for i in movable:
            extra = min(bound - holding[i], max(1, remaining * weights[i] // whole), spare)
            holding[i] = holding[i] + extra
            spare = spare - extra
    return np.array(holding)


def centred(key, shape, deviation, reach, cuts=(), kind=jnp.bfloat16):
    gain = steps_of(key, shape, cuts, -0.22, 0.18) if cuts else 1.0
    entries = jax.random.normal(key, shape, jnp.float32) * deviation * gain
    return jnp.minimum(jnp.maximum(entries, -reach), reach).astype(kind)


def gaussian_with(rng, dims, spread, bound, shards, heavy, held_as=jnp.bfloat16):
    drawn = spread * jax.random.normal(rng, dims, jnp.float32)
    if shards:
        drawn = drawn * steps_of(rng, dims, shards, -0.22, 0.18)
    return jnp.clip(raised(drawn, jax.random.fold_in(rng, 3), *heavy), -bound, bound).astype(held_as)


def setup_inputs(seed: int = 0) -> dict:
    streams_of = jax.random.split(jax.random.key(seed), 7)
    queries = draw_queries(jax.random.fold_in(streams_of[6], 71), 0)
    keys = draw_keys(jax.random.fold_in(streams_of[6], 71), 0)
    values = centred(streams_of[2], (TOKENS, HD), 1.0, 6.0, ((0, 8), (1, 4)))
    bucket_keys = jax.random.split(jax.random.fold_in(streams_of[3], 1), TOKENS // TOK_DEV)
    bucket_turns = jax.random.permutation(jax.random.fold_in(streams_of[3], 3), TOKENS // TOK_DEV)
    bucket = jax.vmap(lambda own, number: assign_block(jax.random.fold_in(streams_of[3], 2), own, number, TOK_DEV, N_SEQ, 1, CAP, 2))(bucket_keys, bucket_turns).reshape((TOKENS, 1))
    w_out = centred(streams_of[4], (HD, D), HD ** -0.5, 0.125, ((0, 4),))
    grad_out = gaussian_with(streams_of[5], (TOKENS, D), 1.0, 6.0, ((0, 8),), (0, 1, 8, 2.0))
    return dict(queries=queries, keys=keys, values=values, bucket=bucket, w_out=w_out, grad_out=grad_out)


def member_table(bucket_grid, owner, slot_count):
    matches = (bucket_grid == owner).astype(jnp.int32)
    ranking = jnp.cumsum(matches, axis=1) - matches
    slot_ids = jnp.arange(slot_count, dtype=jnp.int32)
    placed = matches[:, :, None] * (ranking[:, :, None] == slot_ids[None, None, :]).astype(jnp.int32)
    sources = bucket_grid.shape[0]
    stride = bucket_grid.shape[1]
    offsets = jnp.arange(sources, dtype=jnp.int32)[:, None] * stride + jnp.arange(stride, dtype=jnp.int32)[None, :]
    where_at = lax.optimization_barrier(jnp.sum(placed * offsets[:, :, None], axis=1)).reshape(-1)
    present = lax.optimization_barrier(jnp.sum(placed, axis=1)).reshape(-1)
    return (where_at, present)

def allowed_mask(where_here, alive_here, where_before, alive_before):
    amount = where_here.shape[0]
    asking = alive_here[:, None] > 0
    inside = (where_here[None, :] <= where_here[:, None]) & (alive_here[None, :] > 0) & asking
    inside = inside | (jnp.arange(amount)[:, None] == jnp.arange(amount)[None, :])
    earlier = (where_before[None, :] <= where_here[:, None]) & (alive_before[None, :] > 0) & asking
    return jnp.concatenate([inside, earlier], axis=1)

def softmax_rows(scores, allowed):
    masked = jnp.where(allowed[None], scores, -1e+30)
    largest = lax.optimization_barrier(jnp.max(masked, axis=2, keepdims=True))
    weights = jnp.where(allowed[None], jnp.exp(masked - largest), 0.0)
    return weights / lax.optimization_barrier(jnp.sum(weights, axis=2, keepdims=True))

def reference(queries, keys, values, bucket, w_out, grad_out):
    scaling = 1.0 / math.sqrt(HSZ)
    bucket_grid = bucket[:, 0].reshape(N_SEQ, TOK_DEV)
    grad_heads = jnp.dot(grad_out, w_out.T, preferred_element_type=jnp.float32).astype(jnp.bfloat16)

    def gather_rows(source, where_at, present):
        return jnp.take(source, where_at, axis=0) * present[:, None].astype(source.dtype)

    def split_heads(block):
        return block.astype(jnp.float32).reshape(block.shape[0], HEADS, HSZ)

    def flatten(block):
        return block.reshape(block.shape[0], HEADS * HSZ)

    def bucket_pass(owner):
        where_here, alive_here = member_table(bucket_grid, owner, CAP)
        where_before, alive_before = member_table(bucket_grid, owner - 1, CAP)
        allowed = allowed_mask(where_here, alive_here, where_before, alive_before)
        query_rows = split_heads(gather_rows(queries, where_here, alive_here))
        key_all = split_heads(jnp.concatenate([gather_rows(keys, where_here, alive_here), gather_rows(keys, where_before, alive_before)], axis=0))
        value_all = split_heads(jnp.concatenate([gather_rows(values, where_here, alive_here), gather_rows(values, where_before, alive_before)], axis=0))
        grad_rows = split_heads(gather_rows(grad_heads, where_here, alive_here))
        scores = jnp.einsum('qhd,khd->hqk', query_rows, key_all) * scaling
        probs = softmax_rows(scores, allowed)
        rounded = lax.optimization_barrier(probs.astype(jnp.bfloat16)).astype(jnp.float32)
        attended = jnp.einsum('hqk,khd->qhd', rounded, value_all).astype(jnp.bfloat16)
        centre = lax.optimization_barrier(jnp.sum(attended.astype(jnp.float32) * grad_rows, axis=2))
        dprobs = jnp.einsum('qhd,khd->hqk', grad_rows, value_all)
        dscores = probs * (dprobs - jnp.transpose(centre)[:, :, None])
        dround = lax.optimization_barrier(dscores.astype(jnp.bfloat16)).astype(jnp.float32)
        grad_query = (jnp.einsum('hqk,khd->qhd', dround, key_all) * scaling).astype(jnp.bfloat16)
        grad_key = jnp.einsum('hqk,qhd->khd', dround, query_rows) * scaling
        grad_value = jnp.einsum('hqk,qhd->khd', rounded, grad_rows)
        slot_total = where_here.shape[0]
        return (flatten(attended), flatten(grad_query), flatten(grad_key[:slot_total]), flatten(grad_value[:slot_total]), flatten(grad_key[slot_total:]).astype(jnp.bfloat16), flatten(grad_value[slot_total:]).astype(jnp.bfloat16))
    outcome = lax.map(bucket_pass, jnp.arange(N_SEQ, dtype=jnp.int32))
    attended_all, query_all, key_own, value_own, key_prev, value_prev = outcome
    nothing = jnp.zeros_like(key_prev[:1])
    key_next = jnp.concatenate([key_prev[1:], nothing], axis=0)
    value_next = jnp.concatenate([value_prev[1:], nothing], axis=0)
    key_total = (key_own + key_next.astype(jnp.float32)).astype(jnp.bfloat16)
    value_total = (value_own + value_next.astype(jnp.float32)).astype(jnp.bfloat16)
    owners = jnp.arange(N_SEQ, dtype=jnp.int32)
    onehot = (bucket_grid[:, :, None] == owners[None, None, :]).astype(jnp.int32)
    ranking = lax.optimization_barrier(jnp.sum((jnp.cumsum(onehot, axis=1) - onehot) * onehot, axis=2))
    sources = jnp.arange(N_SEQ, dtype=jnp.int32)[:, None]
    lookup = (bucket_grid * (N_SEQ * CAP) + sources * CAP + ranking).reshape(-1).astype(jnp.int32)

    def collect(stacked):
        return jnp.take(stacked.reshape(-1, HEADS * HSZ), lookup, axis=0)
    attended_tok = collect(attended_all)
    layer_out = jnp.dot(attended_tok, w_out, preferred_element_type=jnp.float32).astype(jnp.bfloat16)
    grad_weight = jnp.dot(attended_tok.T, grad_out, preferred_element_type=jnp.float32)
    return (layer_out, collect(query_all), collect(key_total), collect(value_total), grad_weight)
```

```python
import functools
import math

import jax
import jax.numpy as jnp
from jax import lax
from jax.experimental import pallas as pl
from jax.experimental.pallas import tpu as pltpu
from jax.sharding import PartitionSpec as P

HSZ = 128


def passed_along(value, axis, by):
    length = lax.axis_size(axis)
    pairs = [(i, i + by) for i in range(length) if 0 <= i + by < length]
    return lax.ppermute(value, axis, pairs)


def member_table(bucket_grid, owner, slot_count):
    matches = (bucket_grid == owner).astype(jnp.int32)
    ranking = jnp.cumsum(matches, axis=1) - matches
    slot_ids = jnp.arange(slot_count, dtype=jnp.int32)
    placed = matches[:, :, None] * (ranking[:, :, None] == slot_ids[None, None, :]).astype(
        jnp.int32
    )
    sources = bucket_grid.shape[0]
    stride = bucket_grid.shape[1]
    offsets = (
        jnp.arange(sources, dtype=jnp.int32)[:, None] * stride
        + jnp.arange(stride, dtype=jnp.int32)[None, :]
    )
    where_at = jnp.sum(placed * offsets[:, :, None], axis=1).reshape(-1)
    present = jnp.sum(placed, axis=1).reshape(-1)
    return (where_at, present)


def allowed_mask(where_here, alive_here, where_before, alive_before):
    amount = where_here.shape[0]
    asking = alive_here[:, None] > 0
    inside = (where_here[None, :] <= where_here[:, None]) & (alive_here[None, :] > 0) & asking
    inside = inside | (jnp.arange(amount)[:, None] == jnp.arange(amount)[None, :])
    earlier = (where_before[None, :] <= where_here[:, None]) & (alive_before[None, :] > 0) & asking
    return jnp.concatenate([inside, earlier], axis=1)


def softmax_rows(scores, allowed):
    masked = jnp.where(allowed[None], scores, -1e30)
    largest = jnp.max(masked, axis=2, keepdims=True)
    weights = jnp.where(allowed[None], jnp.exp(masked - largest), 0.0)
    return weights / jnp.sum(weights, axis=2, keepdims=True)


def local_slots(bucket_grid, device, sources, slot_total):
    my_buckets = lax.dynamic_index_in_dim(bucket_grid, device, 0, keepdims=False)
    owners = jnp.arange(sources, dtype=jnp.int32)
    onehot = (my_buckets[:, None] == owners[None, :]).astype(jnp.int32)
    ranking = jnp.sum((jnp.cumsum(onehot, axis=0) - onehot) * onehot, axis=1)
    back_index = my_buckets * slot_total + ranking
    slot_ids = jnp.arange(slot_total, dtype=jnp.int32)
    placed = onehot[:, :, None] * (ranking[:, None, None] == slot_ids[None, None, :]).astype(
        jnp.int32
    )
    token_ids = jnp.arange(my_buckets.shape[0], dtype=jnp.int32)
    send_index = jnp.sum(placed * token_ids[:, None, None], axis=0).reshape(-1)
    send_live = jnp.sum(placed, axis=0).reshape(-1)
    return (back_index, send_index, send_live)


def owner_probs(query_rows, key_all, allowed, scaling):
    scores = (
        jnp.einsum("qgd,kgd->gqk", query_rows, key_all, preferred_element_type=jnp.float32)
        * scaling
    )
    return softmax_rows(scores, allowed)


def owner_forward(probs, value_all):
    rounded = probs.astype(jnp.bfloat16)
    attended = jnp.einsum(
        "gqk,kgd->qgd", rounded, value_all, preferred_element_type=jnp.float32
    ).astype(jnp.bfloat16)
    return (rounded, attended)


def owner_backward(probs, rounded, attended, grad_rows, query_rows, key_all, value_all, scaling):
    centre = jnp.sum(attended.astype(jnp.float32) * grad_rows.astype(jnp.float32), axis=2)
    dprobs = jnp.einsum("qgd,kgd->gqk", grad_rows, value_all, preferred_element_type=jnp.float32)
    dscores = probs * (dprobs - jnp.transpose(centre)[:, :, None])
    dround = dscores.astype(jnp.bfloat16)
    grad_query = (
        jnp.einsum("gqk,kgd->qgd", dround, key_all, preferred_element_type=jnp.float32) * scaling
    ).astype(jnp.bfloat16)
    grad_key = (
        jnp.einsum("gqk,qgd->kgd", dround, query_rows, preferred_element_type=jnp.float32) * scaling
    )
    grad_value = jnp.einsum("gqk,qgd->kgd", rounded, grad_rows, preferred_element_type=jnp.float32)
    return (grad_query, grad_key, grad_value)


def with_previous(key_rows, value_rows):
    key_before, value_before = passed_along((key_rows, value_rows), "seq", 1)
    return (
        jnp.concatenate([key_rows, key_before], axis=0),
        jnp.concatenate([value_rows, value_before], axis=0),
    )


def settle_keys(grad_key, grad_value, slot_rows):
    key_next, value_next = passed_along(
        (grad_key[slot_rows:].astype(jnp.bfloat16), grad_value[slot_rows:].astype(jnp.bfloat16)),
        "seq",
        -1,
    )
    key_total = (grad_key[:slot_rows] + key_next.astype(jnp.float32)).astype(jnp.bfloat16)
    value_total = (grad_value[:slot_rows] + value_next.astype(jnp.float32)).astype(jnp.bfloat16)
    return (key_total, value_total)


def per_device(queries, keys, values, bucket, w_out, grad_out):
    sources = lax.axis_size("seq")
    device = lax.axis_index("seq")
    token_rows = queries.shape[0]
    features = queries.shape[1]
    groups = features // HSZ
    slot_total = max(2, 3 * token_rows // (2 * sources))
    slot_rows = sources * slot_total
    scaling = 1.0 / math.sqrt(HSZ)
    bucket_grid = bucket[:, 0].reshape(sources, token_rows)
    back_index, send_index, send_live = local_slots(bucket_grid, device, sources, slot_total)
    where_here, alive_here = member_table(bucket_grid, device, slot_total)
    where_before, alive_before = member_table(bucket_grid, device - 1, slot_total)
    allowed = allowed_mask(where_here, alive_here, where_before, alive_before)
    grad_heads = lax.dot_general(
        grad_out, w_out, (((1,), (1,)), ((), ())), preferred_element_type=jnp.float32
    ).astype(jnp.bfloat16)

    def pack_rows(source):
        return jnp.take(source, send_index, axis=0) * send_live[:, None].astype(source.dtype)

    def split_heads(block):
        return block.reshape(block.shape[0], groups, HSZ)

    def flatten(block):
        return block.reshape(block.shape[0], features)

    query_rows, key_rows, value_rows = (
        lax.all_to_all(pack_rows(queries), "seq", split_axis=0, concat_axis=0, tiled=True),
        lax.all_to_all(pack_rows(keys), "seq", split_axis=0, concat_axis=0, tiled=True),
        lax.all_to_all(pack_rows(values), "seq", split_axis=0, concat_axis=0, tiled=True),
    )
    key_all, value_all = with_previous(key_rows, value_rows)
    probs = owner_probs(split_heads(query_rows), split_heads(key_all), allowed, scaling)
    rounded, attended = owner_forward(probs, split_heads(value_all))
    key_all, value_all, probs, rounded, attended = (key_all, value_all, probs, rounded, attended)
    returned = lax.all_to_all(flatten(attended), "seq", split_axis=0, concat_axis=0, tiled=True)
    grad_rows = lax.all_to_all(
        pack_rows(grad_heads), "seq", split_axis=0, concat_axis=0, tiled=True
    )
    grad_query, grad_key, grad_value = owner_backward(
        probs,
        rounded,
        attended,
        split_heads(grad_rows),
        split_heads(query_rows),
        split_heads(key_all),
        split_heads(value_all),
        scaling,
    )
    key_total, value_total = settle_keys(flatten(grad_key), flatten(grad_value), slot_rows)
    back_query, back_key, back_value = (
        lax.all_to_all(flatten(grad_query), "seq", split_axis=0, concat_axis=0, tiled=True),
        lax.all_to_all(key_total, "seq", split_axis=0, concat_axis=0, tiled=True),
        lax.all_to_all(value_total, "seq", split_axis=0, concat_axis=0, tiled=True),
    )
    attended_home = jnp.take(returned, back_index, axis=0)
    partial_value = jnp.dot(attended_home, w_out, preferred_element_type=jnp.float32)
    layer_out = lax.psum_scatter(
        partial_value.astype(jnp.bfloat16), "head", scatter_dimension=1, tiled=True
    )
    weight_terms = lax.dot_general(
        attended_home, grad_out, (((0,), (0,)), ((), ())), preferred_element_type=jnp.float32
    )
    grad_weight = lax.psum_scatter(weight_terms, "seq", scatter_dimension=1, tiled=True)
    grad_queries = jnp.take(back_query, back_index, axis=0)
    grad_keys = jnp.take(back_key, back_index, axis=0)
    grad_values = jnp.take(back_value, back_index, axis=0)
    return (layer_out, grad_queries, grad_keys, grad_values, grad_weight)


MESH = pl.DeviceIdType.MESH
NT = (((1,), (1,)), ((), ()))
TN = (((0,), (0,)), ((), ()))


def times(a, b, dims):
    return lax.dot_general(a, b, dims, preferred_element_type=jnp.float32)


def dense_kernel(
    seqs,
    heads,
    q_hbm,
    k_hbm,
    v_hbm,
    bcol,
    brow,
    w_hbm,
    go_hbm,
    lo_out,
    gq_out,
    gk_out,
    gv_out,
    gw_out,
    w_buf,
    go_buf,
    gh_buf,
    q_buf,
    g_buf,
    k_buf,
    v_buf,
    go_all,
    att_all,
    dq_send,
    dk_acc,
    dv_acc,
    dk_send,
    dv_send,
    dq_in,
    dk_in,
    dv_in,
    dk_far,
    dv_far,
    lo_send,
    lo_in,
    local_sem,
    in_send,
    in_recv,
    far_send,
    far_recv,
    go_send,
    go_recv,
    gx_send,
    gx_recv,
    att_send,
    att_recv,
    attx_send,
    attx_recv,
    fwd_send,
    fwd_recv,
    dq_ssem,
    dq_rsem,
    dk_ssem,
    dk_rsem,
    dkf_ssem,
    dkf_rsem,
    lo_ssem,
    lo_rsem,
):
    s = lax.axis_index("seq")
    h = lax.axis_index("head")
    rows = q_hbm.shape[0]
    width = HSZ
    groups = q_hbm.shape[1] // width
    half = lax.div(s, groups)
    mine = lax.rem(s, groups)
    part = groups * rows
    scaling = 1.0 / math.sqrt(HSZ)
    gcols = w_hbm.shape[1] // seqs
    lcols = w_hbm.shape[1] // heads
    quarter = rows // heads
    low = half == 0
    high = half == 1

    def near(r):
        return lax.rem(mine + r, groups)

    def rows_of(block):
        return pl.ds(pl.multiple_of(block * rows, rows), rows)

    def cols_of(block, size=width):
        return pl.ds(pl.multiple_of(block * size, size), size)

    def remote(src, dst, ssem, rsem, where):
        return pltpu.make_async_remote_copy(
            src_ref=src, dst_ref=dst, send_sem=ssem, recv_sem=rsem, device_id=where,
            device_id_type=MESH,
        )

    w_copy = pltpu.make_async_copy(w_hbm, w_buf, local_sem.at[0])
    go_copy = pltpu.make_async_copy(go_hbm, go_buf, local_sem.at[1])
    go_copy.start()
    w_copy.start()
    own = [
        pltpu.make_async_copy(k_hbm.at[:, cols_of(mine)], k_buf.at[rows_of(s), :], local_sem.at[2]),
        pltpu.make_async_copy(v_hbm.at[:, cols_of(mine)], v_buf.at[rows_of(s), :], local_sem.at[3]),
        pltpu.make_async_copy(q_hbm.at[:, cols_of(mine)], q_buf.at[rows_of(mine), :], local_sem.at[4]),
    ]
    for copy in own:
        copy.start()
    quarter_rows = pl.ds(pl.multiple_of(h * quarter, quarter), quarter)
    go_own = pltpu.make_async_copy(
        go_hbm.at[quarter_rows, cols_of(s, gcols)], go_all.at[s, quarter_rows, :], local_sem.at[5]
    )
    go_own.start()

    barrier = pltpu.get_barrier_semaphore()
    for r in range(1, seqs):
        pl.semaphore_signal(
            barrier, inc=1, device_id=(lax.rem(s + r, seqs), h), device_id_type=MESH
        )
    for r in range(1, heads):
        pl.semaphore_signal(
            barrier, inc=1, device_id=(s, lax.rem(h + r, heads)), device_id_type=MESH
        )
    pl.semaphore_wait(barrier, seqs + heads - 2)

    far = []
    for r in range(groups):
        to = near(r)
        there = ((1 - half) * groups + to, h)
        for n, (src, dst) in enumerate(((k_hbm, k_buf), (v_hbm, v_buf))):
            far.append(
                remote(
                    src.at[:, cols_of(to)], dst.at[rows_of(s), :], far_send.at[r, n],
                    far_recv.at[r, n], there,
                )
            )

    inside = []
    for r in range(1, groups):
        to = near(r)
        there = (half * groups + to, h)
        for n, (src, dst, at) in enumerate(
            ((k_hbm, k_buf, s), (v_hbm, v_buf, s), (q_hbm, q_buf, mine))
        ):
            copy = remote(
                src.at[:, cols_of(to)], dst.at[rows_of(at), :], in_send.at[r, n],
                in_recv.at[r, n], there,
            )
            copy.start()
            inside.append(copy)

    @pl.when(low)
    def _():
        for copy in far:
            copy.start()
        k_buf[pl.ds(part, part), :] = jnp.zeros((part, width), k_buf.dtype)
        v_buf[pl.ds(part, part), :] = jnp.zeros((part, width), v_buf.dtype)

    @pl.when(high)
    def _():
        dk_far[...] = jnp.zeros_like(dk_far)
        dv_far[...] = jnp.zeros_like(dv_far)

    go_copy.wait()
    w_copy.wait()
    depth = w_buf.shape[1] // seqs

    def heads_step(c, total):
        at = pl.ds(pl.multiple_of(c * depth, depth), depth)
        return total + times(go_buf[:, at], w_buf[:, at], NT)

    gh = lax.fori_loop(
        0, seqs, heads_step, jnp.zeros((rows, groups * width), jnp.float32)
    )
    gh_buf[...] = gh.astype(jnp.bfloat16)
    for r in range(1, groups):
        to = near(r)
        copy = remote(
            gh_buf.at[:, cols_of(to)], g_buf.at[rows_of(mine), :], in_send.at[r, 3],
            in_recv.at[r, 3], (half * groups + to, h),
        )
        copy.start()
        inside.append(copy)
    g_buf[rows_of(mine), :] = gh_buf[:, cols_of(mine)]

    spread = []
    for r in range(1, seqs):
        to = lax.rem(s + r, seqs)
        copy = remote(
            go_hbm.at[quarter_rows, cols_of(to, gcols)], go_all.at[s, quarter_rows, :],
            go_send.at[r], go_recv.at[r], (to, h),
        )
        copy.start()
        spread.append(copy)

    for copy in own:
        copy.wait()
    for copy in inside:
        copy.wait_recv()

    @pl.when(high)
    def _():
        for copy in far:
            copy.wait_recv()

    keys_bucket = brow[...]
    keys_at = lax.broadcasted_iota(jnp.int32, (rows, seqs * rows), 1)
    exchange = []
    sent = []
    att_near = []
    att_cross = []
    dq_near = []
    order = list(range(1, groups)) + [0]
    for step, r in enumerate(order):
        block = near(r)
        token = half * groups + block
        qc = q_buf[rows_of(block), :]
        gc = g_buf[rows_of(block), :]
        k_all = k_buf[...]
        v_all = v_buf[...]
        gap = bcol[rows_of(token), :] - keys_bucket
        query_at = token * rows + lax.broadcasted_iota(jnp.int32, (rows, seqs * rows), 0)
        allowed = ((gap == 0) | (gap == 1)) & (keys_at <= query_at)
        scores = jnp.where(allowed, times(qc, k_all, NT) * scaling, -1e30)
        largest = jnp.max(scores, axis=1, keepdims=True)
        weights = jnp.where(allowed, jnp.exp(scores - largest), 0.0)
        probs = weights * (1.0 / jnp.sum(weights, axis=1, keepdims=True))
        rounded = probs.astype(jnp.bfloat16)
        attended = jnp.dot(rounded, v_all, preferred_element_type=jnp.float32).astype(jnp.bfloat16)
        att_all[rows_of(token), cols_of(mine)] = attended
        for n in range(1, groups):
            copy = remote(
                att_all.at[rows_of(token), cols_of(mine)],
                att_all.at[rows_of(token), cols_of(mine)],
                att_send.at[step, n], att_recv.at[step, n],
                (half * groups + near(n), h),
            )
            copy.start()
            att_near.append(copy)
        copy = remote(
            att_all.at[rows_of(token), cols_of(mine)],
            att_all.at[rows_of(token), cols_of(mine)],
            attx_send.at[step], attx_recv.at[step], ((1 - half) * groups + mine, h),
        )
        copy.start()
        att_cross.append(copy)
        centre = jnp.sum(
            attended.astype(jnp.float32) * gc.astype(jnp.float32), axis=1, keepdims=True
        )
        dscores = (probs * (times(gc, v_all, NT) - centre)).astype(jnp.bfloat16)
        dq = (jnp.dot(dscores, k_all, preferred_element_type=jnp.float32) * scaling).astype(
            jnp.bfloat16
        )
        if r == 0:
            dq_in[:, cols_of(mine)] = dq
        else:
            dq_send[r] = dq
            copy = remote(
                dq_send.at[r], dq_in.at[:, cols_of(mine)], dq_ssem.at[r], dq_rsem.at[r],
                (token, h),
            )
            copy.start()
            dq_near.append(copy)
        dk = times(dscores, qc, TN)
        dv = times(rounded, gc, TN)
        if step == 0:
            dk_acc[...] = dk
            dv_acc[...] = dv
        else:
            dk_acc[...] += dk
            dv_acc[...] += dv
        if step == 1:
            go_own.wait()
            for copy in spread:
                copy.wait_recv()
            for n in range(1, heads):
                copy = remote(
                    go_all.at[:, quarter_rows, :], go_all.at[:, quarter_rows, :],
                    gx_send.at[n], gx_recv.at[n], (s, lax.rem(h + n, heads)),
                )
                copy.start()
                exchange.append(copy)

    dk_send[...] = (dk_acc[...] * scaling).astype(jnp.bfloat16)
    dv_send[...] = dv_acc[...].astype(jnp.bfloat16)
    dk_cross = []
    for r in range(groups):
        to = near(r)
        for n, (src, dst) in enumerate(((dk_send, dk_far), (dv_send, dv_far))):
            dk_cross.append(
                remote(
                    src.at[rows_of(to), :], dst.at[:, cols_of(mine)], dkf_ssem.at[r, n],
                    dkf_rsem.at[r, n], ((1 - half) * groups + to, h),
                )
            )

    @pl.when(high)
    def _():
        for copy in dk_cross:
            copy.start()

    dk_near = []
    for r in range(1, groups):
        to = near(r)
        for n, (src, dst) in enumerate(((dk_send, dk_in), (dv_send, dv_in))):
            copy = remote(
                src.at[rows_of(half * groups + to), :], dst.at[:, cols_of(mine)],
                dk_ssem.at[r, n], dk_rsem.at[r, n], (half * groups + to, h),
            )
            copy.start()
            dk_near.append(copy)
    dk_in[:, cols_of(mine)] = dk_send[rows_of(s), :]
    dv_in[:, cols_of(mine)] = dv_send[rows_of(s), :]

    for copy in att_cross:
        copy.wait_recv()
    forward = []
    theirs = pl.ds(pl.multiple_of((1 - half) * part, part), part)
    for n in range(1, groups):
        copy = remote(
            att_all.at[theirs, cols_of(mine)], att_all.at[theirs, cols_of(mine)],
            fwd_send.at[n], fwd_recv.at[n], (half * groups + near(n), h),
        )
        copy.start()
        forward.append(copy)

    for copy in att_near:
        copy.wait_recv()
    home = att_all[rows_of(s), :]
    lo_near = []
    for n in range(1, heads):
        to = lax.rem(h + n, heads)
        lo_send[n] = jnp.dot(
            home, w_buf[:, cols_of(to, lcols)], preferred_element_type=jnp.float32
        ).astype(jnp.bfloat16)
        copy = remote(lo_send.at[n], lo_in.at[n], lo_ssem.at[n], lo_rsem.at[n], (s, to))
        copy.start()
        lo_near.append(copy)
    layer = jnp.dot(home, w_buf[:, cols_of(h, lcols)], preferred_element_type=jnp.float32)

    for copy in exchange:
        copy.wait_recv()
    for copy in dq_near:
        copy.wait_recv()
    gq_out[...] = dq_in[...]
    for n, copy in enumerate(lo_near):
        copy.wait_recv()
        layer = layer + lo_in[n + 1].astype(jnp.float32)
    lo_out[...] = layer.astype(jnp.bfloat16)
    for copy in forward:
        copy.wait_recv()
    gw = jnp.zeros(gw_out.shape, jnp.float32)
    for c in range(seqs):
        gw = gw + times(att_all[c * rows : (c + 1) * rows, :], go_all[c], TN)
    gw_out[...] = gw
    for copy in dk_near:
        copy.wait_recv()

    @pl.when(low)
    def _():
        for copy in dk_cross:
            copy.wait_recv()

    gk_out[...] = (dk_in[...].astype(jnp.float32) + dk_far[...].astype(jnp.float32)).astype(
        jnp.bfloat16
    )
    gv_out[...] = (dv_in[...].astype(jnp.float32) + dv_far[...].astype(jnp.float32)).astype(
        jnp.bfloat16
    )

    for copy in (
        inside + spread + exchange + att_near + att_cross + dq_near + dk_near + forward + lo_near
    ):
        copy.wait_send()

    @pl.when(low)
    def _():
        for copy in far:
            copy.wait_send()

    @pl.when(high)
    def _():
        for copy in dk_cross:
            copy.wait_send()


def dense_device(queries, keys, values, bucket, w_out, grad_out):
    seqs = lax.axis_size("seq")
    heads = lax.axis_size("head")
    rows, features = queries.shape
    model = w_out.shape[1]
    groups = features // HSZ
    part = groups * rows
    tokens = seqs * rows
    bf, f32 = jnp.bfloat16, jnp.float32
    vmem = pl.BlockSpec(memory_space=pltpu.VMEM)
    hbm = pl.BlockSpec(memory_space=pl.ANY)
    dma = pltpu.SemaphoreType.DMA
    wide = pltpu.VMEM((rows, features), bf)
    sems = []
    for shape in (
        (groups, 4), (groups, 2), (seqs,), (heads,), (groups, groups), (groups,), (groups,),
        (groups,), (groups, 2), (groups, 2), (heads,),
    ):
        sems += [dma(shape), dma(shape)]
    return pl.pallas_call(
        functools.partial(dense_kernel, seqs, heads),
        out_shape=(
            jax.ShapeDtypeStruct((rows, model // heads), bf),
            jax.ShapeDtypeStruct((rows, features), bf),
            jax.ShapeDtypeStruct((rows, features), bf),
            jax.ShapeDtypeStruct((rows, features), bf),
            jax.ShapeDtypeStruct((features, model // seqs), f32),
        ),
        in_specs=[hbm, hbm, hbm, vmem, vmem, hbm, hbm],
        out_specs=(vmem,) * 5,
        scratch_shapes=[
            pltpu.VMEM(w_out.shape, bf),
            pltpu.VMEM(grad_out.shape, bf),
            wide,
            pltpu.VMEM((part, HSZ), bf),
            pltpu.VMEM((part, HSZ), bf),
            pltpu.VMEM((tokens, HSZ), bf),
            pltpu.VMEM((tokens, HSZ), bf),
            pltpu.VMEM((seqs, rows, model // seqs), bf),
            pltpu.VMEM((tokens, features), bf),
            pltpu.VMEM((groups, rows, HSZ), bf),
            pltpu.VMEM((tokens, HSZ), f32),
            pltpu.VMEM((tokens, HSZ), f32),
            pltpu.VMEM((tokens, HSZ), bf),
            pltpu.VMEM((tokens, HSZ), bf),
            wide,
            wide,
            wide,
            wide,
            wide,
            pltpu.VMEM((heads, rows, model // heads), bf),
            pltpu.VMEM((heads, rows, model // heads), bf),
            dma((6,)),
        ]
        + sems,
        compiler_params=pltpu.CompilerParams(collective_id=0, has_side_effects=True),
    )(queries, keys, values, bucket, bucket.reshape(1, -1), w_out, grad_out)


def choose(queries, keys, values, bucket, w_out, grad_out):
    groups = queries.shape[1] // HSZ
    dense = lax.axis_size("seq") == 2 * groups
    plan = dense_device if dense else per_device
    return plan(queries, keys, values, bucket, w_out, grad_out)


def solution(mesh):
    return jax.shard_map(
        choose,
        mesh=mesh,
        in_specs=(
            P("seq", "head"),
            P("seq", "head"),
            P("seq", "head"),
            P(),
            P("head", None),
            P("seq", None),
        ),
        out_specs=(
            P("seq", "head"),
            P("seq", "head"),
            P("seq", "head"),
            P("seq", "head"),
            P("head", "seq"),
        ),
        check_vma=False,
    )
```

```python
import functools
import math

import jax
import jax.numpy as jnp
from jax import lax
from jax.experimental import pallas as pl
from jax.experimental.pallas import tpu as pltpu
from jax.sharding import PartitionSpec as P

HSZ = 128


def passed_along(value, axis, by):
    length = lax.axis_size(axis)
    pairs = [(i, i + by) for i in range(length) if 0 <= i + by < length]
    return lax.ppermute(value, axis, pairs)


def member_table(bucket_grid, owner, slot_count):
    matches = (bucket_grid == owner).astype(jnp.int32)
    ranking = jnp.cumsum(matches, axis=1) - matches
    slot_ids = jnp.arange(slot_count, dtype=jnp.int32)
    placed = matches[:, :, None] * (ranking[:, :, None] == slot_ids[None, None, :]).astype(
        jnp.int32
    )
    sources = bucket_grid.shape[0]
    stride = bucket_grid.shape[1]
    offsets = (
        jnp.arange(sources, dtype=jnp.int32)[:, None] * stride
        + jnp.arange(stride, dtype=jnp.int32)[None, :]
    )
    where_at = jnp.sum(placed * offsets[:, :, None], axis=1).reshape(-1)
    present = jnp.sum(placed, axis=1).reshape(-1)
    return (where_at, present)


def allowed_mask(where_here, alive_here, where_before, alive_before):
    amount = where_here.shape[0]
    asking = alive_here[:, None] > 0
    inside = (where_here[None, :] <= where_here[:, None]) & (alive_here[None, :] > 0) & asking
    inside = inside | (jnp.arange(amount)[:, None] == jnp.arange(amount)[None, :])
    earlier = (where_before[None, :] <= where_here[:, None]) & (alive_before[None, :] > 0) & asking
    return jnp.concatenate([inside, earlier], axis=1)


def softmax_rows(scores, allowed):
    masked = jnp.where(allowed[None], scores, -1e30)
    largest = jnp.max(masked, axis=2, keepdims=True)
    weights = jnp.where(allowed[None], jnp.exp(masked - largest), 0.0)
    return weights / jnp.sum(weights, axis=2, keepdims=True)


def local_slots(bucket_grid, device, sources, slot_total):
    my_buckets = lax.dynamic_index_in_dim(bucket_grid, device, 0, keepdims=False)
    owners = jnp.arange(sources, dtype=jnp.int32)
    onehot = (my_buckets[:, None] == owners[None, :]).astype(jnp.int32)
    ranking = jnp.sum((jnp.cumsum(onehot, axis=0) - onehot) * onehot, axis=1)
    back_index = my_buckets * slot_total + ranking
    slot_ids = jnp.arange(slot_total, dtype=jnp.int32)
    placed = onehot[:, :, None] * (ranking[:, None, None] == slot_ids[None, None, :]).astype(
        jnp.int32
    )
    token_ids = jnp.arange(my_buckets.shape[0], dtype=jnp.int32)
    send_index = jnp.sum(placed * token_ids[:, None, None], axis=0).reshape(-1)
    send_live = jnp.sum(placed, axis=0).reshape(-1)
    return (back_index, send_index, send_live)


def owner_probs(query_rows, key_all, allowed, scaling):
    scores = (
        jnp.einsum("qgd,kgd->gqk", query_rows, key_all, preferred_element_type=jnp.float32)
        * scaling
    )
    return softmax_rows(scores, allowed)


def owner_forward(probs, value_all):
    rounded = probs.astype(jnp.bfloat16)
    attended = jnp.einsum(
        "gqk,kgd->qgd", rounded, value_all, preferred_element_type=jnp.float32
    ).astype(jnp.bfloat16)
    return (rounded, attended)


def owner_backward(probs, rounded, attended, grad_rows, query_rows, key_all, value_all, scaling):
    centre = jnp.sum(attended.astype(jnp.float32) * grad_rows.astype(jnp.float32), axis=2)
    dprobs = jnp.einsum("qgd,kgd->gqk", grad_rows, value_all, preferred_element_type=jnp.float32)
    dscores = probs * (dprobs - jnp.transpose(centre)[:, :, None])
    dround = dscores.astype(jnp.bfloat16)
    grad_query = (
        jnp.einsum("gqk,kgd->qgd", dround, key_all, preferred_element_type=jnp.float32) * scaling
    ).astype(jnp.bfloat16)
    grad_key = (
        jnp.einsum("gqk,qgd->kgd", dround, query_rows, preferred_element_type=jnp.float32) * scaling
    )
    grad_value = jnp.einsum("gqk,qgd->kgd", rounded, grad_rows, preferred_element_type=jnp.float32)
    return (grad_query, grad_key, grad_value)


def with_previous(key_rows, value_rows):
    key_before, value_before = passed_along((key_rows, value_rows), "seq", 1)
    return (
        jnp.concatenate([key_rows, key_before], axis=0),
        jnp.concatenate([value_rows, value_before], axis=0),
    )


def settle_keys(grad_key, grad_value, slot_rows):
    key_next, value_next = passed_along(
        (grad_key[slot_rows:].astype(jnp.bfloat16), grad_value[slot_rows:].astype(jnp.bfloat16)),
        "seq",
        -1,
    )
    key_total = (grad_key[:slot_rows] + key_next.astype(jnp.float32)).astype(jnp.bfloat16)
    value_total = (grad_value[:slot_rows] + value_next.astype(jnp.float32)).astype(jnp.bfloat16)
    return (key_total, value_total)


def per_device(queries, keys, values, bucket, w_out, grad_out):
    sources = lax.axis_size("seq")
    device = lax.axis_index("seq")
    token_rows = queries.shape[0]
    features = queries.shape[1]
    groups = features // HSZ
    slot_total = max(2, 3 * token_rows // (2 * sources))
    slot_rows = sources * slot_total
    scaling = 1.0 / math.sqrt(HSZ)
    bucket_grid = bucket[:, 0].reshape(sources, token_rows)
    back_index, send_index, send_live = local_slots(bucket_grid, device, sources, slot_total)
    where_here, alive_here = member_table(bucket_grid, device, slot_total)
    where_before, alive_before = member_table(bucket_grid, device - 1, slot_total)
    allowed = allowed_mask(where_here, alive_here, where_before, alive_before)
    grad_heads = lax.dot_general(
        grad_out, w_out, (((1,), (1,)), ((), ())), preferred_element_type=jnp.float32
    ).astype(jnp.bfloat16)

    def pack_rows(source):
        return jnp.take(source, send_index, axis=0) * send_live[:, None].astype(source.dtype)

    def split_heads(block):
        return block.reshape(block.shape[0], groups, HSZ)

    def flatten(block):
        return block.reshape(block.shape[0], features)

    query_rows, key_rows, value_rows = (
        lax.all_to_all(pack_rows(queries), "seq", split_axis=0, concat_axis=0, tiled=True),
        lax.all_to_all(pack_rows(keys), "seq", split_axis=0, concat_axis=0, tiled=True),
        lax.all_to_all(pack_rows(values), "seq", split_axis=0, concat_axis=0, tiled=True),
    )
    key_all, value_all = with_previous(key_rows, value_rows)
    probs = owner_probs(split_heads(query_rows), split_heads(key_all), allowed, scaling)
    rounded, attended = owner_forward(probs, split_heads(value_all))
    key_all, value_all, probs, rounded, attended = (key_all, value_all, probs, rounded, attended)
    returned = lax.all_to_all(flatten(attended), "seq", split_axis=0, concat_axis=0, tiled=True)
    grad_rows = lax.all_to_all(
        pack_rows(grad_heads), "seq", split_axis=0, concat_axis=0, tiled=True
    )
    grad_query, grad_key, grad_value = owner_backward(
        probs,
        rounded,
        attended,
        split_heads(grad_rows),
        split_heads(query_rows),
        split_heads(key_all),
        split_heads(value_all),
        scaling,
    )
    key_total, value_total = settle_keys(flatten(grad_key), flatten(grad_value), slot_rows)
    back_query, back_key, back_value = (
        lax.all_to_all(flatten(grad_query), "seq", split_axis=0, concat_axis=0, tiled=True),
        lax.all_to_all(key_total, "seq", split_axis=0, concat_axis=0, tiled=True),
        lax.all_to_all(value_total, "seq", split_axis=0, concat_axis=0, tiled=True),
    )
    attended_home = jnp.take(returned, back_index, axis=0)
    partial_value = jnp.dot(attended_home, w_out, preferred_element_type=jnp.float32)
    layer_out = lax.psum_scatter(
        partial_value.astype(jnp.bfloat16), "head", scatter_dimension=1, tiled=True
    )
    weight_terms = lax.dot_general(
        attended_home, grad_out, (((0,), (0,)), ((), ())), preferred_element_type=jnp.float32
    )
    grad_weight = lax.psum_scatter(weight_terms, "seq", scatter_dimension=1, tiled=True)
    grad_queries = jnp.take(back_query, back_index, axis=0)
    grad_keys = jnp.take(back_key, back_index, axis=0)
    grad_values = jnp.take(back_value, back_index, axis=0)
    return (layer_out, grad_queries, grad_keys, grad_values, grad_weight)


MESH = pl.DeviceIdType.MESH
NT = (((1,), (1,)), ((), ()))
TN = (((0,), (0,)), ((), ()))


def times(a, b, dims):
    return lax.dot_general(a, b, dims, preferred_element_type=jnp.float32)


def dense_kernel(
    seqs,
    heads,
    q_hbm,
    k_hbm,
    v_hbm,
    brow,
    w_hbm,
    go_hbm,
    lo_out,
    gq_out,
    gk_out,
    gv_out,
    gw_out,
    w_buf,
    go_buf,
    gh_buf,
    q_buf,
    g_buf,
    k_near,
    v_near,
    k_far,
    v_far,
    go_all,
    att_all,
    s_buf,
    dp_buf,
    p_near,
    p_far,
    ds_near,
    ds_far,
    dq_send,
    dk_send,
    dv_send,
    dkf_send,
    dvf_send,
    dq_in,
    dk_in,
    dv_in,
    dk_back,
    dv_back,
    lo_send,
    lo_in,
    sum_send,
    sum_in,
    local_sem,
    in_send,
    in_recv,
    far_send,
    far_recv,
    go_send,
    go_recv,
    gx_send,
    gx_recv,
    gf_send,
    gf_recv,
    att_send,
    att_recv,
    attx_send,
    attx_recv,
    fwd_send,
    fwd_recv,
    dq_ssem,
    dq_rsem,
    dk_ssem,
    dk_rsem,
    dkf_ssem,
    dkf_rsem,
    lo_ssem,
    lo_rsem,
    sum_ssem,
    sum_rsem,
):
    s = lax.axis_index("seq")
    h = lax.axis_index("head")
    bf, f32 = jnp.bfloat16, jnp.float32
    rows = q_hbm.shape[0]
    width = HSZ
    groups = q_hbm.shape[1] // width
    half = lax.div(s, groups)
    mine = lax.rem(s, groups)
    part = groups * rows
    pairs = heads // 2
    core = lax.rem(h, 2)
    partner = h + 1 - 2 * core
    scaling = 1.0 / math.sqrt(HSZ)
    gcols = w_hbm.shape[1] // seqs
    lcols = w_hbm.shape[1] // heads
    quarter = rows // heads
    low = half == 0
    high = half == 1

    def near(r):
        return lax.rem(mine + r, groups)

    def rows_of(block):
        return pl.ds(pl.multiple_of(block * rows, rows), rows)

    def cols_of(block, size=width):
        return pl.ds(pl.multiple_of(block * size, size), size)

    def quarter_of(head):
        return pl.ds(pl.multiple_of(head * quarter, quarter), quarter)

    def remote(src, dst, ssem, rsem, where):
        return pltpu.make_async_remote_copy(
            src_ref=src, dst_ref=dst, send_sem=ssem, recv_sem=rsem, device_id=where,
            device_id_type=MESH,
        )

    w_copy = pltpu.make_async_copy(w_hbm, w_buf, local_sem.at[0])
    go_copy = pltpu.make_async_copy(go_hbm, go_buf, local_sem.at[1])
    go_copy.start()
    w_copy.start()
    own = [
        pltpu.make_async_copy(
            src.at[:, cols_of(mine)], dst.at[rows_of(mine), :], local_sem.at[2 + n]
        )
        for n, (src, dst) in enumerate(((k_hbm, k_near), (v_hbm, v_near), (q_hbm, q_buf)))
    ]
    for copy in own:
        copy.start()
    go_own = pltpu.make_async_copy(
        go_hbm.at[quarter_of(h), cols_of(s, gcols)], go_all.at[s, quarter_of(h), :],
        local_sem.at[5],
    )
    go_own.start()

    barrier = pltpu.get_barrier_semaphore()
    for r in range(1, seqs):
        pl.semaphore_signal(
            barrier, inc=1, device_id=(lax.rem(s + r, seqs), h), device_id_type=MESH
        )
    for r in range(1, heads):
        pl.semaphore_signal(
            barrier, inc=1, device_id=(s, lax.rem(h + r, heads)), device_id_type=MESH
        )
    pl.semaphore_wait(barrier, seqs + heads - 2)

    far = []
    for n, (src, dst) in enumerate(((k_hbm, k_far), (v_hbm, v_far))):
        for r in range(groups):
            to = near(r)
            far.append(
                remote(
                    src.at[:, cols_of(to)], dst.at[rows_of(mine), :], far_send.at[r, n],
                    far_recv.at[r, n], ((1 - half) * groups + to, h),
                )
            )

    @pl.when(low)
    def _():
        for copy in far:
            copy.start()

    inside = []
    for n, (src, dst) in enumerate(((k_hbm, k_near), (q_hbm, q_buf), (v_hbm, v_near))):
        for r in range(1, groups):
            to = near(r)
            copy = remote(
                src.at[:, cols_of(to)], dst.at[rows_of(mine), :], in_send.at[r, n],
                in_recv.at[r, n], (half * groups + to, h),
            )
            copy.start()
            inside.append(copy)

    @pl.when(high)
    def _():
        dk_back[...] = jnp.zeros_like(dk_back)
        dv_back[...] = jnp.zeros_like(dv_back)

    go_copy.wait()
    w_copy.wait()
    depth = w_buf.shape[1] // seqs

    def heads_step(c, total):
        at = pl.ds(pl.multiple_of(c * depth, depth), depth)
        return total + times(go_buf[:, at], w_buf[:, at], NT)

    gh = lax.fori_loop(0, seqs, heads_step, jnp.zeros((rows, groups * width), f32))
    gh_buf[...] = gh.astype(bf)
    inside_g = []
    for r in range(1, groups):
        to = near(r)
        copy = remote(
            gh_buf.at[:, cols_of(to)], g_buf.at[rows_of(mine), :], in_send.at[r, 3],
            in_recv.at[r, 3], (half * groups + to, h),
        )
        copy.start()
        inside_g.append(copy)
    g_buf[rows_of(mine), :] = gh_buf[:, cols_of(mine)]

    spread = []
    for r in range(1, seqs):
        to = lax.rem(s + r, seqs)
        copy = remote(
            go_hbm.at[quarter_of(h), cols_of(to, gcols)], go_all.at[s, quarter_of(h), :],
            go_send.at[r], go_recv.at[r], (to, h),
        )
        copy.start()
        spread.append(copy)

    lanes = lax.broadcasted_iota(jnp.int32, (rows, rows), 1)
    downs = lax.broadcasted_iota(jnp.int32, (rows, rows), 0)

    def asking(token):
        row = brow[:, cols_of(token, rows)]
        return jnp.sum(jnp.where(lanes == downs, row, 0), axis=1, keepdims=True)

    def matching(token, start):
        gap = asking(token) - brow[:, cols_of(start, part)]
        return (gap == 0) | (gap == 1)

    for copy in own:
        copy.wait()
    for copy in inside:
        copy.wait_recv()

    order = list(range(1, groups)) + [0]
    keys_at = lax.broadcasted_iota(jnp.int32, (rows, part), 1)
    query_at = lax.broadcasted_iota(jnp.int32, (rows, part), 0)
    for r in order:
        block = near(r)
        allowed = matching(half * groups + block, half) & (keys_at <= block * rows + query_at)
        s_buf[rows_of(block), :] = jnp.where(
            allowed, times(q_buf[rows_of(block), :], k_near[...], NT) * scaling, -1e30
        )
    for copy in inside_g:
        copy.wait_recv()
    for r in order:
        at = rows_of(near(r))
        dp_buf[at, :] = times(g_buf[at, :], v_near[...], NT)

    att_near, att_cross, dq_near, dk_near, dk_cross, exchange = [], [], [], [], [], []
    for step, r in enumerate(order):
        token = half * groups + near(r)
        piece = att_all.at[rows_of(token), cols_of(mine)]
        att_near.append(
            [
                remote(
                    piece, piece, att_send.at[step, n], att_recv.at[step, n],
                    (half * groups + near(n), h),
                )
                for n in range(1, groups)
            ]
        )
        att_cross.append(
            remote(
                piece, piece, attx_send.at[step], attx_recv.at[step],
                ((1 - half) * groups + mine, h),
            )
        )
        if r > 0:
            dq_near.append(
                remote(
                    dq_send.at[r], dq_in.at[:, cols_of(mine)], dq_ssem.at[r], dq_rsem.at[r],
                    (token, h),
                )
            )
            for n, (src, dst) in enumerate(((dk_send, dk_in), (dv_send, dv_in))):
                dk_near.append(
                    remote(
                        src.at[rows_of(near(r)), :], dst.at[:, cols_of(mine)], dk_ssem.at[r, n],
                        dk_rsem.at[r, n], (token, h),
                    )
                )
        for n, (src, dst) in enumerate(((dkf_send, dk_back), (dvf_send, dv_back))):
            dk_cross.append(
                remote(
                    src.at[rows_of(near(r)), :], dst.at[:, cols_of(mine)], dkf_ssem.at[r, n],
                    dkf_rsem.at[r, n], ((1 - half) * groups + near(r), h),
                )
            )

    def finish(with_far):
        for step, r in enumerate(order):
            block = near(r)
            at = rows_of(block)
            qc, gc = q_buf[at, :], g_buf[at, :]
            scores = s_buf[at, :]
            largest = jnp.max(scores, axis=1, keepdims=True)
            if with_far:
                others = jnp.where(
                    matching(groups + block, 0), times(qc, k_far[...], NT) * scaling, -1e30
                )
                largest = jnp.maximum(largest, jnp.max(others, axis=1, keepdims=True))
            weights = jnp.exp(scores - largest)
            total = jnp.sum(weights, axis=1, keepdims=True)
            if with_far:
                more = jnp.exp(others - largest)
                total = total + jnp.sum(more, axis=1, keepdims=True)
            share = 1.0 / total
            probs = weights * share
            rounded = probs.astype(bf)
            attended = jnp.dot(rounded, v_near[...], preferred_element_type=f32)
            p_near[at, :] = rounded
            if with_far:
                probs_far = more * share
                rounded_far = probs_far.astype(bf)
                attended = attended + jnp.dot(
                    rounded_far, v_far[...], preferred_element_type=f32
                )
                p_far[at, :] = rounded_far
            attended = attended.astype(bf)
            att_all[rows_of(half * groups + block), cols_of(mine)] = attended
            att_cross[step].start()
            for copy in att_near[step]:
                copy.start()
            centre = jnp.sum(attended.astype(f32) * gc.astype(f32), axis=1, keepdims=True)
            ds_near[at, :] = (probs * (dp_buf[at, :] - centre)).astype(bf)
            if with_far:
                ds_far[at, :] = (probs_far * (times(gc, v_far[...], NT) - centre)).astype(bf)
        if with_far:
            for step, r in enumerate(order):
                at = rows_of(near(r))
                dvf_send[at, :] = times(p_far[:, cols_of(near(r), rows)], g_buf[...], TN).astype(bf)
                dkf_send[at, :] = (
                    times(ds_far[:, cols_of(near(r), rows)], q_buf[...], TN) * scaling
                ).astype(bf)
                dk_cross[2 * step].start()
                dk_cross[2 * step + 1].start()
        for step, r in enumerate(order):
            at = rows_of(near(r))
            dq = jnp.dot(ds_near[at, :], k_near[...], preferred_element_type=f32)
            if with_far:
                dq = dq + jnp.dot(ds_far[at, :], k_far[...], preferred_element_type=f32)
            dq = (dq * scaling).astype(bf)
            dv = times(p_near[:, cols_of(near(r), rows)], g_buf[...], TN).astype(bf)
            dk = (times(ds_near[:, cols_of(near(r), rows)], q_buf[...], TN) * scaling).astype(bf)
            if r == 0:
                dq_in[:, cols_of(mine)] = dq
                dk_in[:, cols_of(mine)] = dk
                dv_in[:, cols_of(mine)] = dv
            else:
                dq_send[r] = dq
                dk_send[at, :] = dk
                dv_send[at, :] = dv
                dq_near[step].start()
                dk_near[2 * step].start()
                dk_near[2 * step + 1].start()

    @pl.when(low)
    def _():
        finish(False)

    @pl.when(high)
    def _():
        for copy in far:
            copy.wait_recv()
        finish(True)

    go_own.wait()
    for copy in spread:
        copy.wait_recv()
    level = go_all.at[:, quarter_of(h), :]
    for m in range(1, pairs):
        exchange.append(
            remote(
                level, level, gx_send.at[m], gx_recv.at[m], (s, lax.rem(h + 2 * m, heads))
            )
        )
        exchange[-1].start()
    passing = [remote(level, level, gf_send.at[0], gf_recv.at[0], (s, partner))]
    passing[0].start()

    for copies in att_near:
        for copy in copies:
            copy.wait_recv()
    home = att_all[rows_of(s), :]

    def product(to):
        return jnp.dot(home, w_buf[:, cols_of(to, lcols)], preferred_element_type=f32)

    def same_core(m):
        return lax.rem(h + 2 * m, heads)

    def other_core(m):
        return lax.rem(h - core + 2 * m, heads) + 1 - core

    lo_near = []
    for m in list(range(1, pairs)) + [0]:
        lo_send[m] = product(other_core(m)).astype(bf)
        copy = remote(lo_send.at[m], lo_in.at[m], lo_ssem.at[m], lo_rsem.at[m], (s, partner))
        copy.start()
        lo_near.append(copy)

    for copy in att_cross:
        copy.wait_recv()
    forward = []
    theirs = pl.ds(pl.multiple_of((1 - half) * part, part), part)
    for n in range(1, groups):
        copy = remote(
            att_all.at[theirs, cols_of(mine)], att_all.at[theirs, cols_of(mine)],
            fwd_send.at[n], fwd_recv.at[n], (half * groups + near(n), h),
        )
        copy.start()
        forward.append(copy)

    sums = []
    for m in range(1, pairs):
        mixed = product(same_core(m))
        lo_near[m - 1].wait_recv()
        sum_send[m] = (mixed + lo_in[m].astype(f32)).astype(bf)
        copy = remote(
            sum_send.at[m], sum_in.at[m], sum_ssem.at[m], sum_rsem.at[m], (s, same_core(m))
        )
        copy.start()
        sums.append(copy)
    layer = product(h)

    for m in range(1, pairs):
        exchange[m - 1].wait_recv()
        from_there = go_all.at[:, quarter_of(lax.rem(h + heads - 2 * m, heads)), :]
        copy = remote(from_there, from_there, gf_send.at[m], gf_recv.at[m], (s, partner))
        copy.start()
        passing.append(copy)

    for copy in dq_near:
        copy.wait_recv()
    gq_out[...] = dq_in[...]
    for copy in passing:
        copy.wait_recv()
    for copy in forward:
        copy.wait_recv()
    gw = jnp.zeros(gw_out.shape, f32)
    for c in range(seqs):
        gw = gw + times(att_all[c * rows : (c + 1) * rows, :], go_all[c], TN)
    gw_out[...] = gw
    lo_near[-1].wait_recv()
    layer = layer + lo_in[0].astype(f32)
    for m in range(1, pairs):
        sums[m - 1].wait_recv()
        layer = layer + sum_in[m].astype(f32)
    lo_out[...] = layer.astype(bf)
    for copy in dk_near:
        copy.wait_recv()

    @pl.when(low)
    def _():
        for copy in dk_cross:
            copy.wait_recv()

    gk_out[...] = (dk_in[...].astype(f32) + dk_back[...].astype(f32)).astype(bf)
    gv_out[...] = (dv_in[...].astype(f32) + dv_back[...].astype(f32)).astype(bf)

    for copy in (
        inside + inside_g + spread + exchange + passing + sum(att_near, []) + att_cross + dq_near
        + dk_near + forward + lo_near + sums
    ):
        copy.wait_send()

    @pl.when(low)
    def _():
        for copy in far:
            copy.wait_send()

    @pl.when(high)
    def _():
        for copy in dk_cross:
            copy.wait_send()


def hand_over(count, *refs):
    sources, targets, holds = refs[:count], refs[count : 2 * count], refs[2 * count : 3 * count]
    sem_in, sem_out = refs[3 * count :]
    fetched = [
        pltpu.make_async_copy(a, b, sem_in.at[n]) for n, (a, b) in enumerate(zip(sources, holds))
    ]
    written = [
        pltpu.make_async_copy(a, b, sem_out.at[n]) for n, (a, b) in enumerate(zip(holds, targets))
    ]
    for copy in fetched:
        copy.start()
    for one, two in zip(fetched, written):
        one.wait()
        two.start()
    for copy in written:
        copy.wait()


def dense_device(queries, keys, values, bucket, w_out, grad_out):
    seqs = lax.axis_size("seq")
    heads = lax.axis_size("head")
    rows, features = queries.shape
    model = w_out.shape[1]
    groups = features // HSZ
    pairs = heads // 2
    part = groups * rows
    tokens = seqs * rows
    bf, f32 = jnp.bfloat16, jnp.float32
    vmem = pl.BlockSpec(memory_space=pltpu.VMEM)
    hbm = pl.BlockSpec(memory_space=pl.ANY)
    dma = pltpu.SemaphoreType.DMA
    wide = pltpu.VMEM((rows, features), bf)
    tall = pltpu.VMEM((part, HSZ), bf)
    square = pltpu.VMEM((part, part), bf)
    layers = pltpu.VMEM((pairs, rows, model // heads), bf)
    sems = []
    for shape in (
        (groups, 4), (groups, 2), (seqs,), (pairs,), (pairs,), (groups, groups), (groups,),
        (groups,), (groups,), (groups, 2), (groups, 2), (pairs,), (pairs,),
    ):
        sems += [dma(shape), dma(shape)]
    results = (
        jax.ShapeDtypeStruct((rows, model // heads), bf),
        jax.ShapeDtypeStruct((rows, features), bf),
        jax.ShapeDtypeStruct((rows, features), bf),
        jax.ShapeDtypeStruct((rows, features), bf),
        jax.ShapeDtypeStruct((features, model // seqs), f32),
    )
    outs = pl.pallas_call(
        functools.partial(dense_kernel, seqs, heads),
        out_shape=results,
        in_specs=[hbm, hbm, hbm, vmem, hbm, hbm],
        out_specs=(vmem,) * 5,
        scratch_shapes=[
            pltpu.VMEM(w_out.shape, bf),
            pltpu.VMEM(grad_out.shape, bf),
            wide,
            *([tall] * 6),
            pltpu.VMEM((seqs, rows, model // seqs), bf),
            pltpu.VMEM((tokens, features), bf),
            pltpu.VMEM((part, part), f32),
            pltpu.VMEM((part, part), f32),
            *([square] * 4),
            pltpu.VMEM((groups, rows, HSZ), bf),
            *([tall] * 4),
            *([wide] * 5),
            *([layers] * 4),
            dma((6,)),
        ]
        + sems,
        compiler_params=pltpu.CompilerParams(collective_id=0, has_side_effects=True),
    )(queries, keys, values, bucket.reshape(1, -1), w_out, grad_out)
    return pl.pallas_call(
        functools.partial(hand_over, len(results)),
        out_shape=results,
        in_specs=[hbm] * len(results),
        out_specs=(hbm,) * len(results),
        scratch_shapes=[pltpu.VMEM(r.shape, r.dtype) for r in results]
        + [dma((len(results),)), dma((len(results),))],
    )(*outs)


def choose(queries, keys, values, bucket, w_out, grad_out):
    groups = queries.shape[1] // HSZ
    dense = lax.axis_size("seq") == 2 * groups and lax.axis_size("head") % 2 == 0
    plan = dense_device if dense else per_device
    return plan(queries, keys, values, bucket, w_out, grad_out)


def solution(mesh):
    return jax.shard_map(
        choose,
        mesh=mesh,
        in_specs=(
            P("seq", "head"),
            P("seq", "head"),
            P("seq", "head"),
            P(),
            P("head", None),
            P("seq", None),
        ),
        out_specs=(
            P("seq", "head"),
            P("seq", "head"),
            P("seq", "head"),
            P("seq", "head"),
            P("head", "seq"),
        ),
        check_vma=False,
    )
```

```python
import functools
import math

import jax
import jax.numpy as jnp
from jax import lax
from jax.experimental import pallas as pl
from jax.experimental.pallas import tpu as pltpu
from jax.sharding import PartitionSpec as P

HSZ = 128


def passed_along(value, axis, by):
    length = lax.axis_size(axis)
    pairs = [(i, i + by) for i in range(length) if 0 <= i + by < length]
    return lax.ppermute(value, axis, pairs)


def member_table(bucket_grid, owner, slot_count):
    matches = (bucket_grid == owner).astype(jnp.int32)
    ranking = jnp.cumsum(matches, axis=1) - matches
    slot_ids = jnp.arange(slot_count, dtype=jnp.int32)
    placed = matches[:, :, None] * (ranking[:, :, None] == slot_ids[None, None, :]).astype(
        jnp.int32
    )
    sources = bucket_grid.shape[0]
    stride = bucket_grid.shape[1]
    offsets = (
        jnp.arange(sources, dtype=jnp.int32)[:, None] * stride
        + jnp.arange(stride, dtype=jnp.int32)[None, :]
    )
    where_at = jnp.sum(placed * offsets[:, :, None], axis=1).reshape(-1)
    present = jnp.sum(placed, axis=1).reshape(-1)
    return (where_at, present)


def allowed_mask(where_here, alive_here, where_before, alive_before):
    amount = where_here.shape[0]
    asking = alive_here[:, None] > 0
    inside = (where_here[None, :] <= where_here[:, None]) & (alive_here[None, :] > 0) & asking
    inside = inside | (jnp.arange(amount)[:, None] == jnp.arange(amount)[None, :])
    earlier = (where_before[None, :] <= where_here[:, None]) & (alive_before[None, :] > 0) & asking
    return jnp.concatenate([inside, earlier], axis=1)


def softmax_rows(scores, allowed):
    masked = jnp.where(allowed[None], scores, -1e30)
    largest = jnp.max(masked, axis=2, keepdims=True)
    weights = jnp.where(allowed[None], jnp.exp(masked - largest), 0.0)
    return weights / jnp.sum(weights, axis=2, keepdims=True)


def local_slots(bucket_grid, device, sources, slot_total):
    my_buckets = lax.dynamic_index_in_dim(bucket_grid, device, 0, keepdims=False)
    owners = jnp.arange(sources, dtype=jnp.int32)
    onehot = (my_buckets[:, None] == owners[None, :]).astype(jnp.int32)
    ranking = jnp.sum((jnp.cumsum(onehot, axis=0) - onehot) * onehot, axis=1)
    back_index = my_buckets * slot_total + ranking
    slot_ids = jnp.arange(slot_total, dtype=jnp.int32)
    placed = onehot[:, :, None] * (ranking[:, None, None] == slot_ids[None, None, :]).astype(
        jnp.int32
    )
    token_ids = jnp.arange(my_buckets.shape[0], dtype=jnp.int32)
    send_index = jnp.sum(placed * token_ids[:, None, None], axis=0).reshape(-1)
    send_live = jnp.sum(placed, axis=0).reshape(-1)
    return (back_index, send_index, send_live)


def owner_probs(query_rows, key_all, allowed, scaling):
    scores = (
        jnp.einsum("qgd,kgd->gqk", query_rows, key_all, preferred_element_type=jnp.float32)
        * scaling
    )
    return softmax_rows(scores, allowed)


def owner_forward(probs, value_all):
    rounded = probs.astype(jnp.bfloat16)
    attended = jnp.einsum(
        "gqk,kgd->qgd", rounded, value_all, preferred_element_type=jnp.float32
    ).astype(jnp.bfloat16)
    return (rounded, attended)


def owner_backward(probs, rounded, attended, grad_rows, query_rows, key_all, value_all, scaling):
    centre = jnp.sum(attended.astype(jnp.float32) * grad_rows.astype(jnp.float32), axis=2)
    dprobs = jnp.einsum("qgd,kgd->gqk", grad_rows, value_all, preferred_element_type=jnp.float32)
    dscores = probs * (dprobs - jnp.transpose(centre)[:, :, None])
    dround = dscores.astype(jnp.bfloat16)
    grad_query = (
        jnp.einsum("gqk,kgd->qgd", dround, key_all, preferred_element_type=jnp.float32) * scaling
    ).astype(jnp.bfloat16)
    grad_key = (
        jnp.einsum("gqk,qgd->kgd", dround, query_rows, preferred_element_type=jnp.float32) * scaling
    )
    grad_value = jnp.einsum("gqk,qgd->kgd", rounded, grad_rows, preferred_element_type=jnp.float32)
    return (grad_query, grad_key, grad_value)


def with_previous(key_rows, value_rows):
    key_before, value_before = passed_along((key_rows, value_rows), "seq", 1)
    return (
        jnp.concatenate([key_rows, key_before], axis=0),
        jnp.concatenate([value_rows, value_before], axis=0),
    )


def settle_keys(grad_key, grad_value, slot_rows):
    key_next, value_next = passed_along(
        (grad_key[slot_rows:].astype(jnp.bfloat16), grad_value[slot_rows:].astype(jnp.bfloat16)),
        "seq",
        -1,
    )
    key_total = (grad_key[:slot_rows] + key_next.astype(jnp.float32)).astype(jnp.bfloat16)
    value_total = (grad_value[:slot_rows] + value_next.astype(jnp.float32)).astype(jnp.bfloat16)
    return (key_total, value_total)


def per_device(queries, keys, values, bucket, w_out, grad_out):
    sources = lax.axis_size("seq")
    device = lax.axis_index("seq")
    token_rows = queries.shape[0]
    features = queries.shape[1]
    groups = features // HSZ
    slot_total = max(2, 3 * token_rows // (2 * sources))
    slot_rows = sources * slot_total
    scaling = 1.0 / math.sqrt(HSZ)
    bucket_grid = bucket[:, 0].reshape(sources, token_rows)
    back_index, send_index, send_live = local_slots(bucket_grid, device, sources, slot_total)
    where_here, alive_here = member_table(bucket_grid, device, slot_total)
    where_before, alive_before = member_table(bucket_grid, device - 1, slot_total)
    allowed = allowed_mask(where_here, alive_here, where_before, alive_before)
    grad_heads = lax.dot_general(
        grad_out, w_out, (((1,), (1,)), ((), ())), preferred_element_type=jnp.float32
    ).astype(jnp.bfloat16)

    def pack_rows(source):
        return jnp.take(source, send_index, axis=0) * send_live[:, None].astype(source.dtype)

    def split_heads(block):
        return block.reshape(block.shape[0], groups, HSZ)

    def flatten(block):
        return block.reshape(block.shape[0], features)

    query_rows, key_rows, value_rows = (
        lax.all_to_all(pack_rows(queries), "seq", split_axis=0, concat_axis=0, tiled=True),
        lax.all_to_all(pack_rows(keys), "seq", split_axis=0, concat_axis=0, tiled=True),
        lax.all_to_all(pack_rows(values), "seq", split_axis=0, concat_axis=0, tiled=True),
    )
    key_all, value_all = with_previous(key_rows, value_rows)
    probs = owner_probs(split_heads(query_rows), split_heads(key_all), allowed, scaling)
    rounded, attended = owner_forward(probs, split_heads(value_all))
    key_all, value_all, probs, rounded, attended = (key_all, value_all, probs, rounded, attended)
    returned = lax.all_to_all(flatten(attended), "seq", split_axis=0, concat_axis=0, tiled=True)
    grad_rows = lax.all_to_all(
        pack_rows(grad_heads), "seq", split_axis=0, concat_axis=0, tiled=True
    )
    grad_query, grad_key, grad_value = owner_backward(
        probs,
        rounded,
        attended,
        split_heads(grad_rows),
        split_heads(query_rows),
        split_heads(key_all),
        split_heads(value_all),
        scaling,
    )
    key_total, value_total = settle_keys(flatten(grad_key), flatten(grad_value), slot_rows)
    back_query, back_key, back_value = (
        lax.all_to_all(flatten(grad_query), "seq", split_axis=0, concat_axis=0, tiled=True),
        lax.all_to_all(key_total, "seq", split_axis=0, concat_axis=0, tiled=True),
        lax.all_to_all(value_total, "seq", split_axis=0, concat_axis=0, tiled=True),
    )
    attended_home = jnp.take(returned, back_index, axis=0)
    partial_value = jnp.dot(attended_home, w_out, preferred_element_type=jnp.float32)
    layer_out = lax.psum_scatter(
        partial_value.astype(jnp.bfloat16), "head", scatter_dimension=1, tiled=True
    )
    weight_terms = lax.dot_general(
        attended_home, grad_out, (((0,), (0,)), ((), ())), preferred_element_type=jnp.float32
    )
    grad_weight = lax.psum_scatter(weight_terms, "seq", scatter_dimension=1, tiled=True)
    grad_queries = jnp.take(back_query, back_index, axis=0)
    grad_keys = jnp.take(back_key, back_index, axis=0)
    grad_values = jnp.take(back_value, back_index, axis=0)
    return (layer_out, grad_queries, grad_keys, grad_values, grad_weight)


MESH = pl.DeviceIdType.MESH
NT = (((1,), (1,)), ((), ()))
TN = (((0,), (0,)), ((), ()))


def times(a, b, dims):
    return lax.dot_general(a, b, dims, preferred_element_type=jnp.float32)


def dense_kernel(
    seqs,
    heads,
    q_hbm,
    k_hbm,
    v_hbm,
    brow,
    w_hbm,
    go_hbm,
    lo_out,
    gq_out,
    gk_out,
    gv_out,
    gw_out,
    w_buf,
    go_buf,
    gh_buf,
    q_buf,
    g_buf,
    k_near,
    v_near,
    k_far,
    v_far,
    go_all,
    att_all,
    s_buf,
    dp_buf,
    p_near,
    p_far,
    ds_near,
    ds_far,
    dq_send,
    dk_send,
    dv_send,
    dkf_send,
    dvf_send,
    dq_in,
    dk_in,
    dv_in,
    dk_back,
    dv_back,
    lo_send,
    lo_in,
    sum_send,
    sum_in,
    local_sem,
    in_send,
    in_recv,
    far_send,
    far_recv,
    go_send,
    go_recv,
    gx_send,
    gx_recv,
    gf_send,
    gf_recv,
    att_send,
    att_recv,
    attx_send,
    attx_recv,
    rel_send,
    rel_recv,
    fwd_send,
    fwd_recv,
    far_rel_send,
    far_rel_recv,
    dq_ssem,
    dq_rsem,
    dk_ssem,
    dk_rsem,
    dkf_ssem,
    dkf_rsem,
    lo_ssem,
    lo_rsem,
    sum_ssem,
    sum_rsem,
):
    s = lax.axis_index("seq")
    h = lax.axis_index("head")
    bf, f32 = jnp.bfloat16, jnp.float32
    rows = q_hbm.shape[0]
    width = HSZ
    groups = q_hbm.shape[1] // width
    half = lax.div(s, groups)
    mine = lax.rem(s, groups)
    part = groups * rows
    pairs = heads // 2
    core = lax.rem(h, 2)
    partner = h + 1 - 2 * core
    scaling = 1.0 / math.sqrt(HSZ)
    gcols = w_hbm.shape[1] // seqs
    lcols = w_hbm.shape[1] // heads
    quarter = rows // heads
    low = half == 0
    high = half == 1

    def near(r):
        return lax.rem(mine + r, groups)

    def rows_of(block):
        return pl.ds(pl.multiple_of(block * rows, rows), rows)

    def cols_of(block, size=width):
        return pl.ds(pl.multiple_of(block * size, size), size)

    def quarter_of(head):
        return pl.ds(pl.multiple_of(head * quarter, quarter), quarter)

    def remote(src, dst, ssem, rsem, where):
        return pltpu.make_async_remote_copy(
            src_ref=src, dst_ref=dst, send_sem=ssem, recv_sem=rsem, device_id=where,
            device_id_type=MESH,
        )

    w_copy = pltpu.make_async_copy(w_hbm, w_buf, local_sem.at[0])
    go_copy = pltpu.make_async_copy(go_hbm, go_buf, local_sem.at[1])
    go_copy.start()
    w_copy.start()
    own = [
        pltpu.make_async_copy(
            src.at[:, cols_of(mine)], dst.at[rows_of(mine), :], local_sem.at[2 + n]
        )
        for n, (src, dst) in enumerate(((k_hbm, k_near), (v_hbm, v_near), (q_hbm, q_buf)))
    ]
    for copy in own:
        copy.start()
    go_own = pltpu.make_async_copy(
        go_hbm.at[quarter_of(h), cols_of(s, gcols)], go_all.at[s, quarter_of(h), :],
        local_sem.at[5],
    )
    go_own.start()

    barrier = pltpu.get_barrier_semaphore()
    for r in range(1, seqs):
        pl.semaphore_signal(
            barrier, inc=1, device_id=(lax.rem(s + r, seqs), h), device_id_type=MESH
        )
    for r in range(1, heads):
        pl.semaphore_signal(
            barrier, inc=1, device_id=(s, lax.rem(h + r, heads)), device_id_type=MESH
        )
    pl.semaphore_wait(barrier, seqs + heads - 2)

    far = []
    for n, (src, dst) in enumerate(((k_hbm, k_far), (v_hbm, v_far))):
        for r in range(groups):
            to = near(r)
            far.append(
                remote(
                    src.at[:, cols_of(to)], dst.at[rows_of(mine), :], far_send.at[r, n],
                    far_recv.at[r, n], ((1 - half) * groups + to, h),
                )
            )

    @pl.when(low)
    def _():
        for copy in far:
            copy.start()

    inside = []
    for n, (src, dst) in enumerate(((k_hbm, k_near), (q_hbm, q_buf), (v_hbm, v_near))):
        for r in range(1, groups):
            to = near(r)
            copy = remote(
                src.at[:, cols_of(to)], dst.at[rows_of(mine), :], in_send.at[r, n],
                in_recv.at[r, n], (half * groups + to, h),
            )
            copy.start()
            inside.append(copy)

    @pl.when(high)
    def _():
        dk_back[...] = jnp.zeros_like(dk_back)
        dv_back[...] = jnp.zeros_like(dv_back)

    go_copy.wait()
    w_copy.wait()
    depth = w_buf.shape[1] // seqs

    def heads_step(c, total):
        at = pl.ds(pl.multiple_of(c * depth, depth), depth)
        return total + times(go_buf[:, at], w_buf[:, at], NT)

    gh = lax.fori_loop(0, seqs, heads_step, jnp.zeros((rows, groups * width), f32))
    for j in range(groups):
        gh_buf[j] = gh[:, j * width : (j + 1) * width].astype(bf)
    inside_g = []
    for r in range(1, groups):
        to = near(r)
        copy = remote(
            gh_buf.at[to], g_buf.at[rows_of(mine), :], in_send.at[r, 3],
            in_recv.at[r, 3], (half * groups + to, h),
        )
        copy.start()
        inside_g.append(copy)
    g_buf[rows_of(mine), :] = gh_buf[mine]

    spread = []
    for r in range(1, seqs):
        to = lax.rem(s + r, seqs)
        copy = remote(
            go_hbm.at[quarter_of(h), cols_of(to, gcols)], go_all.at[s, quarter_of(h), :],
            go_send.at[r], go_recv.at[r], (to, h),
        )
        copy.start()
        spread.append(copy)

    lanes = lax.broadcasted_iota(jnp.int32, (rows, rows), 1)
    downs = lax.broadcasted_iota(jnp.int32, (rows, rows), 0)

    def asking(token):
        row = brow[:, cols_of(token, rows)]
        return jnp.sum(jnp.where(lanes == downs, row, 0), axis=1, keepdims=True)

    def matching(token, start):
        gap = asking(token) - brow[:, cols_of(start, part)]
        return (gap == 0) | (gap == 1)

    for copy in own:
        copy.wait()
    for copy in inside:
        copy.wait_recv()

    order = list(range(1, groups)) + [0]
    keys_at = lax.broadcasted_iota(jnp.int32, (rows, part), 1)
    query_at = lax.broadcasted_iota(jnp.int32, (rows, part), 0)
    for r in order:
        block = near(r)
        allowed = matching(half * groups + block, half) & (keys_at <= block * rows + query_at)
        s_buf[rows_of(block), :] = jnp.where(
            allowed, times(q_buf[rows_of(block), :], k_near[...], NT) * scaling, -1e30
        )
    for copy in inside_g:
        copy.wait_recv()
    for r in order:
        at = rows_of(near(r))
        dp_buf[at, :] = times(g_buf[at, :], v_near[...], NT)

    across = mine + 1 - 2 * lax.rem(mine, 2)
    beside = [across] + [near(2 * k) for k in range(1, groups // 2)]
    att_near, att_cross, dq_near, dk_near, dk_cross, exchange = [], [], [], [], [], []
    for step, r in enumerate(order):
        token = half * groups + near(r)
        piece = att_all.at[mine, rows_of(token), :]
        att_near.append(
            [
                remote(
                    piece, piece, att_send.at[step, n], att_recv.at[step, n],
                    (half * groups + to, h),
                )
                for n, to in enumerate(beside)
            ]
        )
        att_cross.append(
            remote(
                piece, piece, attx_send.at[step], attx_recv.at[step],
                ((1 - half) * groups + mine, h),
            )
        )
        if r > 0:
            dq_near.append(
                remote(
                    dq_send.at[r], dq_in.at[mine], dq_ssem.at[r], dq_rsem.at[r],
                    (token, h),
                )
            )
            for n, (src, dst) in enumerate(((dk_send, dk_in), (dv_send, dv_in))):
                dk_near.append(
                    remote(
                        src.at[rows_of(near(r)), :], dst.at[mine], dk_ssem.at[r, n],
                        dk_rsem.at[r, n], (token, h),
                    )
                )
        for n, (src, dst) in enumerate(((dkf_send, dk_back), (dvf_send, dv_back))):
            dk_cross.append(
                remote(
                    src.at[rows_of(near(r)), :], dst.at[mine], dkf_ssem.at[r, n],
                    dkf_rsem.at[r, n], ((1 - half) * groups + near(r), h),
                )
            )

    def finish(with_far):
        for step, r in enumerate(order):
            block = near(r)
            at = rows_of(block)
            qc, gc = q_buf[at, :], g_buf[at, :]
            scores = s_buf[at, :]
            largest = jnp.max(scores, axis=1, keepdims=True)
            if with_far:
                others = jnp.where(
                    matching(groups + block, 0), times(qc, k_far[...], NT) * scaling, -1e30
                )
                largest = jnp.maximum(largest, jnp.max(others, axis=1, keepdims=True))
            weights = jnp.exp(scores - largest)
            total = jnp.sum(weights, axis=1, keepdims=True)
            if with_far:
                more = jnp.exp(others - largest)
                total = total + jnp.sum(more, axis=1, keepdims=True)
            share = 1.0 / total
            probs = weights * share
            rounded = probs.astype(bf)
            attended = jnp.dot(rounded, v_near[...], preferred_element_type=f32)
            p_near[at, :] = rounded
            if with_far:
                probs_far = more * share
                rounded_far = probs_far.astype(bf)
                attended = attended + jnp.dot(
                    rounded_far, v_far[...], preferred_element_type=f32
                )
                p_far[at, :] = rounded_far
            attended = attended.astype(bf)
            att_all[mine, rows_of(half * groups + block), :] = attended
            att_cross[step].start()
            for copy in att_near[step]:
                copy.start()
            centre = jnp.sum(attended.astype(f32) * gc.astype(f32), axis=1, keepdims=True)
            ds_near[at, :] = (probs * (dp_buf[at, :] - centre)).astype(bf)
            if with_far:
                ds_far[at, :] = (probs_far * (times(gc, v_far[...], NT) - centre)).astype(bf)
        if with_far:
            for step, r in enumerate(order):
                at = rows_of(near(r))
                dvf_send[at, :] = times(p_far[:, cols_of(near(r), rows)], g_buf[...], TN).astype(bf)
                dkf_send[at, :] = (
                    times(ds_far[:, cols_of(near(r), rows)], q_buf[...], TN) * scaling
                ).astype(bf)
                dk_cross[2 * step].start()
                dk_cross[2 * step + 1].start()
        for step, r in enumerate(order):
            at = rows_of(near(r))
            dq = jnp.dot(ds_near[at, :], k_near[...], preferred_element_type=f32)
            if with_far:
                dq = dq + jnp.dot(ds_far[at, :], k_far[...], preferred_element_type=f32)
            dq = (dq * scaling).astype(bf)
            dv = times(p_near[:, cols_of(near(r), rows)], g_buf[...], TN).astype(bf)
            dk = (times(ds_near[:, cols_of(near(r), rows)], q_buf[...], TN) * scaling).astype(bf)
            if r == 0:
                dq_in[mine] = dq
                dk_in[mine] = dk
                dv_in[mine] = dv
            else:
                dq_send[r] = dq
                dk_send[at, :] = dk
                dv_send[at, :] = dv
                dq_near[step].start()
                dk_near[2 * step].start()
                dk_near[2 * step + 1].start()

    @pl.when(low)
    def _():
        finish(False)

    @pl.when(high)
    def _():
        for copy in far:
            copy.wait_recv()
        finish(True)

    go_own.wait()
    for copy in spread:
        copy.wait_recv()
    level = go_all.at[:, quarter_of(h), :]
    for m in range(1, pairs):
        exchange.append(
            remote(
                level, level, gx_send.at[m], gx_recv.at[m], (s, lax.rem(h + 2 * m, heads))
            )
        )
        exchange[-1].start()
    passing = [remote(level, level, gf_send.at[0], gf_recv.at[0], (s, partner))]
    passing[0].start()

    ours = pl.ds(pl.multiple_of(half * part, part), part)
    theirs = pl.ds(pl.multiple_of((1 - half) * part, part), part)

    def block_of(where, column):
        return att_all.at[column, where, :]

    relay = []
    for k in range(1, groups // 2):
        for copies in att_near:
            copies[k].wait_recv()
        block = block_of(ours, near(groups - 2 * k))
        relay.append(
            remote(block, block, rel_send.at[k], rel_recv.at[k], (half * groups + across, h))
        )
        relay[-1].start()
    for copy in att_cross:
        copy.wait_recv()
    forward = []
    for n, to in reversed(list(enumerate(beside))):
        block = block_of(theirs, mine)
        copy = remote(block, block, fwd_send.at[n], fwd_recv.at[n], (half * groups + to, h))
        copy.start()
        forward.append(copy)
    for copies in att_near:
        copies[0].wait_recv()
    for copy in relay:
        copy.wait_recv()
    home = jnp.concatenate([att_all[j, rows_of(s), :] for j in range(groups)], axis=1)

    def product(to):
        return jnp.dot(home, w_buf[:, cols_of(to, lcols)], preferred_element_type=f32)

    def same_core(m):
        return lax.rem(h + 2 * m, heads)

    def other_core(m):
        return lax.rem(h - core + 2 * m, heads) + 1 - core

    lo_near = []
    for m in list(range(1, pairs)) + [0]:
        lo_send[m] = product(other_core(m)).astype(bf)
        copy = remote(lo_send.at[m], lo_in.at[m], lo_ssem.at[m], lo_rsem.at[m], (s, partner))
        copy.start()
        lo_near.append(copy)

    sums = []
    for m in range(1, pairs):
        mixed = product(same_core(m))
        lo_near[m - 1].wait_recv()
        sum_send[m] = (mixed + lo_in[m].astype(f32)).astype(bf)
        copy = remote(
            sum_send.at[m], sum_in.at[m], sum_ssem.at[m], sum_rsem.at[m], (s, same_core(m))
        )
        copy.start()
        sums.append(copy)
    layer = product(h)

    for m in range(1, pairs):
        exchange[m - 1].wait_recv()
        from_there = go_all.at[:, quarter_of(lax.rem(h + heads - 2 * m, heads)), :]
        copy = remote(from_there, from_there, gf_send.at[m], gf_recv.at[m], (s, partner))
        copy.start()
        passing.append(copy)

    far_relay = []
    for k in range(1, groups // 2):
        forward[groups // 2 - 1 - k].wait_recv()
        block = block_of(theirs, near(groups - 2 * k))
        far_relay.append(
            remote(
                block, block, far_rel_send.at[k], far_rel_recv.at[k],
                (half * groups + across, h),
            )
        )
        far_relay[-1].start()

    for copy in dq_near:
        copy.wait_recv()
    for j in range(groups):
        gq_out[:, j * width : (j + 1) * width] = dq_in[j]
    for copy in passing:
        copy.wait_recv()

    def weigh(which):
        at = pl.ds(pl.multiple_of(which * part, part), part)
        grads = go_all[pl.ds(which * groups, groups)].reshape(part, gcols)
        return [times(att_all[j, at, :], grads, TN) for j in range(groups)]

    for j, term in enumerate(weigh(half)):
        gw_out[j * width : (j + 1) * width, :] = term
    forward[-1].wait_recv()
    for copy in far_relay:
        copy.wait_recv()
    for j, term in enumerate(weigh(1 - half)):
        gw_out[j * width : (j + 1) * width, :] += term
    lo_near[-1].wait_recv()
    layer = layer + lo_in[0].astype(f32)
    for m in range(1, pairs):
        sums[m - 1].wait_recv()
        layer = layer + sum_in[m].astype(f32)
    lo_out[...] = layer.astype(bf)
    for copy in dk_near:
        copy.wait_recv()

    @pl.when(low)
    def _():
        for copy in dk_cross:
            copy.wait_recv()

    for j in range(groups):
        at = slice(j * width, (j + 1) * width)
        gk_out[:, at] = (dk_in[j].astype(f32) + dk_back[j].astype(f32)).astype(bf)
        gv_out[:, at] = (dv_in[j].astype(f32) + dv_back[j].astype(f32)).astype(bf)

    for copy in (
        inside + inside_g + spread + exchange + passing + sum(att_near, []) + att_cross + dq_near
        + dk_near + relay + forward + far_relay + lo_near + sums
    ):
        copy.wait_send()

    @pl.when(low)
    def _():
        for copy in far:
            copy.wait_send()

    @pl.when(high)
    def _():
        for copy in dk_cross:
            copy.wait_send()


def hand_over(count, piece, *refs):
    sources, targets, holds = refs[:count], refs[count : 2 * count], refs[2 * count : 3 * count]
    sem_in, sem_out = refs[3 * count :]
    fetched, written = [], []
    for a, b, c in zip(sources, holds, targets):
        for start in range(0, a.shape[0], piece):
            at, n = pl.ds(start, piece), len(fetched)
            fetched.append(pltpu.make_async_copy(a.at[at], b.at[at], sem_in.at[n]))
            written.append(pltpu.make_async_copy(b.at[at], c.at[at], sem_out.at[n]))
    for copy in fetched:
        copy.start()
    for one, two in zip(fetched, written):
        one.wait()
        two.start()
    for copy in written:
        copy.wait()


def dense_device(queries, keys, values, bucket, w_out, grad_out):
    seqs = lax.axis_size("seq")
    heads = lax.axis_size("head")
    rows, features = queries.shape
    model = w_out.shape[1]
    groups = features // HSZ
    pairs = heads // 2
    part = groups * rows
    tokens = seqs * rows
    bf, f32 = jnp.bfloat16, jnp.float32
    vmem = pl.BlockSpec(memory_space=pltpu.VMEM)
    hbm = pl.BlockSpec(memory_space=pl.ANY)
    dma = pltpu.SemaphoreType.DMA
    piled = pltpu.VMEM((groups, rows, HSZ), bf)
    tall = pltpu.VMEM((part, HSZ), bf)
    square = pltpu.VMEM((part, part), bf)
    layers = pltpu.VMEM((pairs, rows, model // heads), bf)
    sems = []
    for shape in (
        (groups, 4), (groups, 2), (seqs,), (pairs,), (pairs,), (groups, groups), (groups,),
        (groups,), (groups,), (groups,), (groups,), (groups, 2), (groups, 2), (pairs,), (pairs,),
    ):
        sems += [dma(shape), dma(shape)]
    results = (
        jax.ShapeDtypeStruct((rows, model // heads), bf),
        jax.ShapeDtypeStruct((rows, features), bf),
        jax.ShapeDtypeStruct((rows, features), bf),
        jax.ShapeDtypeStruct((rows, features), bf),
        jax.ShapeDtypeStruct((features, model // seqs), f32),
    )
    pieces = sum(r.shape[0] // rows for r in results)
    outs = pl.pallas_call(
        functools.partial(dense_kernel, seqs, heads),
        out_shape=results,
        in_specs=[hbm, hbm, hbm, vmem, hbm, hbm],
        out_specs=(vmem,) * 5,
        scratch_shapes=[
            pltpu.VMEM(w_out.shape, bf),
            pltpu.VMEM(grad_out.shape, bf),
            piled,
            *([tall] * 6),
            pltpu.VMEM((seqs, rows, model // seqs), bf),
            pltpu.VMEM((groups, tokens, HSZ), bf),
            pltpu.VMEM((part, part), f32),
            pltpu.VMEM((part, part), f32),
            *([square] * 4),
            pltpu.VMEM((groups, rows, HSZ), bf),
            *([tall] * 4),
            *([piled] * 5),
            *([layers] * 4),
            dma((6,)),
        ]
        + sems,
        compiler_params=pltpu.CompilerParams(collective_id=0, has_side_effects=True),
    )(queries, keys, values, bucket.reshape(1, -1), w_out, grad_out)
    return pl.pallas_call(
        functools.partial(hand_over, len(results), rows),
        out_shape=results,
        in_specs=[hbm] * len(results),
        out_specs=(hbm,) * len(results),
        scratch_shapes=[pltpu.VMEM(r.shape, r.dtype) for r in results]
        + [dma((pieces,)), dma((pieces,))],
    )(*outs)


def choose(queries, keys, values, bucket, w_out, grad_out):
    groups = queries.shape[1] // HSZ
    dense = lax.axis_size("seq") == 2 * groups and lax.axis_size("head") % 2 == 0 and groups % 2 == 0
    plan = dense_device if dense else per_device
    return plan(queries, keys, values, bucket, w_out, grad_out)


def solution(mesh):
    return jax.shard_map(
        choose,
        mesh=mesh,
        in_specs=(
            P("seq", "head"),
            P("seq", "head"),
            P("seq", "head"),
            P(),
            P("head", None),
            P("seq", None),
        ),
        out_specs=(
            P("seq", "head"),
            P("seq", "head"),
            P("seq", "head"),
            P("seq", "head"),
            P("head", "seq"),
        ),
        check_vma=False,
    )
```
